256 devices in a mesh: gx: 4 (over y), gy: 16 (over z, x_lo), ma: 4 (over x_hi, core).
Axes of the slice: x: 4 (x_hi: 2, x_lo: 2; x = x_hi * 2 + x_lo), y: 4, z: 8, core: 2. Of those that a mesh axis runs over, the one named last changes fastest.
Arguments:
- control: float32 [33, 256, 2048], P(None, 'gx', 'gy'), may hold values from -6 to 6
- perturb: bfloat16 [16, 33, 256, 2048], P('ma', None, 'gx', 'gy'), may hold values from -6 to 6
- weights: float32 [16, 256, 2048], P('ma', 'gx', 'gy'), may hold values from -6 to 6
- kappa: float32 [4, 256, 2048], P(None, 'gx', 'gy'), may hold values from 0.2 to 0.49
- wet_levels: int32 [256, 2048], P('gx', 'gy'), may hold values from 0 to 31
- obs_index: int32 [131072], P(('gx', 'gy')), may hold values from 0 to 270335, as said below
- obs_count: int32 [64], P(('gx', 'gy')), may hold values from 1024 to 2048, as said below
- innov: float32 [131072], P(('gx', 'gy')), may hold values from -6 to 6
- obs_weight: float32 [131072], P(('gx', 'gy')), may hold values from 0.25 to 4
Outputs:
- grad_control: float32 [33, 256, 2048], P(None, 'gx', 'gy')
- grad_weights: float32 [16, 256, 2048], P('ma', 'gx', 'gy')
The draws below stay inside these ranges and needn't reach their ends.
Inputs may be any that keep to these rules, and one draw needn't show every extreme that they name: `obs_index`: index p * 64 * 128 + i * 128 + j of a cell of plane p, local longitude i and local latitude j within the observation's tile; several slots may name the same cell. `obs_count`: the live slots of a tile are its first ones. Column (i, j) is wet at level l when l < wet_levels[i, j].
All inputs are finite; a program needn't handle non-finite values.
Results may differ from the reference program's by a relative error of at most 0.0003.
Values sent between devices are 32-bit elements; how exact they have to be, the bound alone decides.
A program may use at most 64 MiB of HBM per device.

```python
import math
import jax
import jax.numpy as jnp
from jax import lax

CX = 64
CY = 128
LEV = 16
OBS_DEV = 2048
NSTEP = 10
LSTEP = 4
PLANES = 33
MEMBERS = 16
TILES = 64
OBS = 131072
NX = 256
NY = 2048
N_GX = 4
N_GY = 16


def draw_obs_index(key, part):
    total = OBS
    top = (2 * LEV + 1) * CX * CY
    values = jax.random.randint(jax.random.fold_in(key, 11), (total,), 0, top)
    first = jax.random.randint(jax.random.fold_in(key, 12), (), 0, total)
    second = (first + 1 + jax.random.randint(jax.random.fold_in(key, 13), (), 0, total - 1)) % total
    positions = jnp.arange(total)
    values = jnp.where(positions == first, top - 1, values)
    values = jnp.where(positions == second, 0, values)
    return values.astype(jnp.int32)


def draw_obs_count(key, part):
    total = TILES
    values = jax.random.randint(jax.random.fold_in(key, 21), (total,), OBS_DEV // 2, OBS_DEV + 1)
    first = jax.random.randint(jax.random.fold_in(key, 22), (), 0, total)
    second = (first + 1 + jax.random.randint(jax.random.fold_in(key, 23), (), 0, total - 1)) % total
    positions = jnp.arange(total)
    values = jnp.where(positions == first, OBS_DEV, values)
    values = jnp.where(positions == second, OBS_DEV // 2, values)
    return values.astype(jnp.int32)


def set_ends(entries, key, smallest, top_value):
    place = [jax.random.randint(jax.random.fold_in(key, axis), (), 0, length) for axis, length in enumerate(entries.shape)]
    main_axis = entries.shape.index(max(entries.shape))
    beside = place[:main_axis] + [(place[main_axis] + 1) % entries.shape[main_axis]] + place[main_axis + 1:]
    return entries.at[tuple(place)].set(smallest).at[tuple(beside)].set(top_value)


def block_levels(rng, shape, cuts, least, top_value):
    def one(position, parts):
        draws = jax.random.uniform(jax.random.fold_in(jax.random.fold_in(rng, 6), position), (parts,), jnp.float32, least / len(cuts), top_value / len(cuts))
        return jnp.repeat(jnp.exp(draws), shape[position] // parts).reshape((-1,) + (1,) * (len(shape) - position - 1))

    factor_of = one(*cuts[0])
    for cut in cuts[1:]:
        factor_of = factor_of * one(*cut)
    return factor_of


def noise(rng, shape, width, most, shards=(), held_as=jnp.bfloat16):
    array = jax.random.normal(rng, shape, jnp.float32) * width
    if len(shards) > 0:
        array = block_levels(rng, shape, shards, -0.22, 0.18) * array
    return jnp.clip(array, min=-most, max=most).astype(held_as)


def setup_inputs(seed: int = 0) -> dict:
    key_list = jax.random.split(jax.random.key(seed), 10)
    return {
        "control": noise(key_list[0], (PLANES, NX, NY), 1.0, 6.0, ((1, 4), (2, 16)), jnp.float32),
        "perturb": noise(key_list[1], (MEMBERS, PLANES, NX, NY), 1.0, 6.0, ((0, 4), (2, 4), (3, 16))),
        "weights": noise(key_list[2], (MEMBERS, NX, NY), 1.0, 6.0, ((0, 4), (1, 4), (2, 16)), jnp.float32),
        "kappa": jnp.clip(jnp.exp(math.log(0.49) - 0.896088 * jax.random.uniform(key_list[3], (4, NX, NY), jnp.float32) ** block_levels(key_list[3], (4, NX, NY), ((1, 4), (2, 16)), -0.2, 0.2)), 0.2, 0.49),
        "wet_levels": set_ends(jax.random.randint(key_list[4], (NX, NY), 0, 2 * LEV), jax.random.fold_in(key_list[4], 1), 0, (2 * LEV) - 1).astype(jnp.int32),
        "obs_index": draw_obs_index(jax.random.fold_in(key_list[9], 71), 0),
        "obs_count": draw_obs_count(jax.random.fold_in(key_list[9], 71), 0),
        "innov": noise(key_list[7], (OBS,), 1.0, 6.0, ((0, 64),), jnp.float32),
        "obs_weight": jnp.clip(jnp.exp(math.log(4.0) - 2.7725887 * jax.random.uniform(key_list[8], (OBS,), jnp.float32) ** block_levels(key_list[8], (OBS,), ((0, 64),), -0.2, 0.2)), 0.25, 4.0),
    }


def coefficients(kappa, wet_levels):
    level_iota = lax.broadcasted_iota(jnp.int32, (LEV, 1, 1), 0)
    wet_mask = (level_iota < wet_levels[None]).astype(jnp.float32)
    surface = wet_mask[0:1]
    return jnp.concatenate([kappa[0:1] * wet_mask, kappa[1:2] * wet_mask, kappa[2:3] * surface, kappa[3:4] * surface], axis=0)

def face_terms(coef):
    face_x = coef * jnp.roll(coef, -1, axis=1)
    inner = coef[:, :, :-1] * coef[:, :, 1:]
    face_y = jnp.concatenate([inner, jnp.zeros_like(coef[:, :, :1])], axis=2)
    return (face_x, face_y)

def one_step(field, face_x, face_y):
    flux_x = face_x * (jnp.roll(field, -1, axis=1) - field)
    change_x = flux_x - jnp.roll(flux_x, 1, axis=1)
    edge = jnp.zeros_like(field[:, :, :1])
    flux_y = face_y * jnp.concatenate([field[:, :, 1:] - field[:, :, :-1], edge], axis=2)
    change_y = flux_y - jnp.concatenate([edge, flux_y[:, :, :-1]], axis=2)
    return field + change_x + change_y

def diffuse(field, face_x, face_y, count):
    return lax.fori_loop(0, count, lambda index, current: one_step(current, face_x, face_y), field)

def to_tiles(field):
    planes = field.shape[0]
    return field.reshape(planes, N_GX, CX, N_GY, CY).transpose(1, 3, 0, 2, 4).reshape(N_GX * N_GY, planes * CX * CY)

def from_tiles(tiles, planes):
    return tiles.reshape(N_GX, N_GY, planes, CX, CY).transpose(2, 0, 3, 1, 4).reshape(planes, N_GX * CX, N_GY * CY)

def reference(control, perturb, weights, kappa, wet_levels, obs_index, obs_count, innov, obs_weight):
    planes = control.shape[0]
    coef = coefficients(kappa, wet_levels)
    face_x, face_y = face_terms(coef)
    static_x, static_y = (face_x[:planes], face_y[:planes])
    local_x, local_y = (face_x[planes:], face_y[planes:])
    member_scale = 1.0 / math.sqrt(MEMBERS)
    static = diffuse(control, static_x, static_y, NSTEP)
    local = diffuse(weights, local_x, local_y, LSTEP)

    def add_member(index, summed):
        return summed + perturb[index].astype(jnp.float32) * local[index][None]
    ensemble = member_scale * lax.fori_loop(0, MEMBERS, add_member, jnp.zeros_like(control))
    state = static + ensemble
    tiles = to_tiles(state)
    obs_cells = obs_index.reshape(TILES, OBS_DEV).astype(jnp.int32)
    observed = jnp.take_along_axis(tiles, obs_cells, axis=1)
    live_obs = lax.broadcasted_iota(jnp.int32, (TILES, OBS_DEV), 1) < obs_count[:, None]
    misfit = obs_weight.reshape(TILES, OBS_DEV) * (observed - innov.reshape(TILES, OBS_DEV))
    resid = jnp.where(live_obs, misfit, jnp.zeros_like(misfit))
    tile_rows = lax.broadcasted_iota(jnp.int32, (TILES, OBS_DEV), 0)
    adjoint_tiles = jnp.zeros_like(tiles).at[tile_rows, obs_cells].add(resid)
    adjoint = from_tiles(adjoint_tiles, planes)
    grad_control = control + diffuse(adjoint, static_x, static_y, NSTEP)
    project = lax.map(lambda member: lax.optimization_barrier(jnp.sum(member.astype(jnp.float32) * adjoint, axis=0)), perturb)
    grad_weights = weights + diffuse(member_scale * project, local_x, local_y, LSTEP)
    return (grad_control, grad_weights)
```

```python
import math

import jax
import jax.numpy as jnp
from jax import lax
from jax.experimental import pallas as pl
from jax.experimental.pallas import tpu as pltpu
from jax.sharding import PartitionSpec as P

NSTEP = 10
LSTEP = 4
HALO = NSTEP


def passed_along(value, axis, steps):
    count = lax.axis_size(axis)
    pairs = [(source, (source + steps) % count) for source in range(count)]
    return lax.ppermute(value, axis, pairs)


def shifted(value, axis, steps):
    count = lax.axis_size(axis)
    initial, last = (max(0, -steps), min(count, count - steps))
    return lax.ppermute(value, axis, [(source, source + steps) for source in range(initial, last)])


def round_up(value, unit):
    return (value + unit - 1) // unit * unit


def extended(field, halo):
    planes, rows, columns = field.shape
    total_rows = round_up(rows + 2 * halo, 8)
    total_columns = round_up(columns + 2 * halo, 128)
    east = passed_along(field[:, :halo, :], "gx", -1)
    west = passed_along(field[:, rows - halo :, :], "gx", 1)
    gap = jnp.zeros((planes, total_rows - rows - 2 * halo, columns), field.dtype)
    wide = jnp.concatenate([field, east, gap, west], axis=1)
    north = shifted(wide[:, :, :halo], "gy", -1)
    south = shifted(wide[:, :, columns - halo :], "gy", 1)
    gap = jnp.zeros((planes, total_rows, total_columns - columns - 2 * halo), field.dtype)
    return jnp.concatenate([wide, north, gap, south], axis=2)


def diffuse_call(ext, first, coef, coef_plane, steps, planes, core, base=None):
    _, rows, columns = ext.shape
    core_rows, core_columns = core

    def kernel(*refs):
        if base is None:
            u_ref, c_ref, o_ref = refs
        else:
            u_ref, c_ref, b_ref, o_ref = refs
        c = c_ref[0]
        face_x = c * pltpu.roll(c, rows - 1, 0)
        face_y = c * pltpu.roll(c, columns - 1, 1)

        def step(index, u):
            flux_x = face_x * (pltpu.roll(u, rows - 1, 0) - u)
            change_x = flux_x - pltpu.roll(flux_x, 1, 0)
            flux_y = face_y * (pltpu.roll(u, columns - 1, 1) - u)
            change_y = flux_y - pltpu.roll(flux_y, 1, 1)
            return u + change_x + change_y

        u = lax.fori_loop(0, steps, step, u_ref[0], unroll=True)
        kept = u[:core_rows, :core_columns]
        if base is None:
            o_ref[0] = kept
        else:
            o_ref[0] = b_ref[0] + kept

    in_specs = [
        pl.BlockSpec((1, rows, columns), lambda p: (p + first, 0, 0)),
        pl.BlockSpec((1, rows, columns), coef_plane),
    ]
    operands = [ext, coef]
    if base is not None:
        in_specs.append(pl.BlockSpec((1, core_rows, core_columns), lambda p: (p, 0, 0)))
        operands.append(base)
    return pl.pallas_call(
        kernel,
        grid=(planes,),
        in_specs=in_specs,
        out_specs=pl.BlockSpec((1, core_rows, core_columns), lambda p: (p, 0, 0)),
        out_shape=jax.ShapeDtypeStruct((planes, core_rows, core_columns), jnp.float32),
    )(*operands)


def on_device(
    control, perturb, weights, kappa, wet_levels, obs_index, obs_count, innov, obs_weight
):
    planes, cells_x, cells_y = control.shape
    members = weights.shape[0]
    levels = (planes - 1) // 2
    core = (cells_x, cells_y)
    stack = jnp.concatenate(
        [control, weights, kappa, wet_levels.astype(jnp.float32)[None]], axis=0
    )
    ext = extended(stack, HALO)
    first_kappa = planes + members
    kappa_ext = ext[first_kappa : first_kappa + 4]
    wet_ext = ext[first_kappa + 4]
    level_iota = lax.broadcasted_iota(jnp.int32, (levels, 1, 1), 0).astype(jnp.float32)
    wet_mask = (level_iota < wet_ext[None]).astype(jnp.float32)
    surface = wet_mask[0:1]
    coef = jnp.concatenate(
        [kappa_ext[0:1] * wet_mask, kappa_ext[1:2] * wet_mask, kappa_ext[2:3] * surface, kappa_ext[3:4] * surface],
        axis=0,
    )
    static_plane = lambda p: (p, 0, 0)
    local_plane = lambda p: (planes, 0, 0)
    member_scale = 1.0 / math.sqrt(members * lax.axis_size("ma"))
    static = diffuse_call(ext, 0, coef, static_plane, NSTEP, planes, core)
    local = diffuse_call(ext, planes, coef, local_plane, LSTEP, members, core)
    partial_sum = member_scale * jnp.sum(perturb.astype(jnp.float32) * local[:, None], axis=0)
    ensemble_seen = lax.psum(partial_sum.reshape(-1)[obs_index], "ma")
    static_seen = static.reshape(-1)[obs_index]
    observed = static_seen + ensemble_seen
    live_obs = lax.broadcasted_iota(jnp.int32, obs_index.shape, 0) < obs_count[0]
    misfit = obs_weight * (observed - innov)
    resid = jnp.where(live_obs, misfit, jnp.zeros_like(misfit))
    adjoint = jnp.zeros((planes * cells_x * cells_y,), jnp.float32).at[obs_index].add(resid)
    adjoint = adjoint.reshape(planes, cells_x, cells_y)
    project = member_scale * jnp.sum(perturb.astype(jnp.float32) * adjoint[None], axis=1)
    ext2 = extended(jnp.concatenate([adjoint, project], axis=0), HALO)
    grad_control = diffuse_call(ext2, 0, coef, static_plane, NSTEP, planes, core, base=control)
    grad_weights = diffuse_call(ext2, planes, coef, local_plane, LSTEP, members, core, base=weights)
    return (grad_control, grad_weights)


def solution(mesh):
    placed = (
        P(None, "gx", "gy"),
        P("ma", None, "gx", "gy"),
        P("ma", "gx", "gy"),
        P(None, "gx", "gy"),
        P("gx", "gy"),
        P(("gx", "gy")),
        P(("gx", "gy")),
        P(("gx", "gy")),
        P(("gx", "gy")),
    )
    return jax.shard_map(
        on_device,
        mesh=mesh,
        in_specs=placed,
        out_specs=(P(None, "gx", "gy"), P("ma", "gx", "gy")),
        check_vma=False,
    )
```

```python
import math

import jax
import jax.numpy as jnp
from jax import lax
from jax.experimental import pallas as pl
from jax.experimental.pallas import tpu as pltpu
from jax.sharding import PartitionSpec as P

NSTEP = 10
LSTEP = 4
HALO = NSTEP


def passed_along(value, axis, steps):
    count = lax.axis_size(axis)
    pairs = [(source, (source + steps) % count) for source in range(count)]
    return lax.ppermute(value, axis, pairs)


def shifted(value, axis, steps):
    count = lax.axis_size(axis)
    initial, last = (max(0, -steps), min(count, count - steps))
    return lax.ppermute(value, axis, [(source, source + steps) for source in range(initial, last)])


def round_up(value, unit):
    return (value + unit - 1) // unit * unit


def received(value, along_x, along_y):
    count_x = lax.axis_size("gx")
    count_y = lax.axis_size("gy")
    pairs = []
    for source_x in range(count_x):
        for source_y in range(count_y):
            target_y = source_y - along_y
            if 0 <= target_y < count_y:
                target_x = (source_x - along_x) % count_x
                pairs.append((source_x * count_y + source_y, target_x * count_y + target_y))
    return lax.ppermute(value, ("gx", "gy"), pairs)


def extended(field, halo):
    planes, rows, columns = field.shape
    total_rows = round_up(rows + 2 * halo, 8)
    total_columns = round_up(columns + 2 * halo, 128)
    first_rows = field[:, :halo]
    last_rows = field[:, rows - halo :]
    east = received(first_rows, 1, 0)
    west = received(last_rows, -1, 0)
    north = received(field[:, :, :halo], 0, 1)
    south = received(field[:, :, columns - halo :], 0, -1)
    east_north = received(first_rows[:, :, :halo], 1, 1)
    east_south = received(first_rows[:, :, columns - halo :], 1, -1)
    west_north = received(last_rows[:, :, :halo], -1, 1)
    west_south = received(last_rows[:, :, columns - halo :], -1, -1)

    def column(middle, after, before):
        width = middle.shape[2]
        gap = jnp.zeros((planes, total_rows - rows - 2 * halo, width), field.dtype)
        return jnp.concatenate([middle, after, gap, before], axis=1)

    gap = jnp.zeros((planes, total_rows, total_columns - columns - 2 * halo), field.dtype)
    return jnp.concatenate(
        [column(field, east, west), column(north, east_north, west_north), gap, column(south, east_south, west_south)],
        axis=2,
    )


def diffuse_call(ext, first, coef, coef_plane, steps, planes, core, base=None):
    _, rows, columns = ext.shape
    core_rows, core_columns = core

    def kernel(*refs):
        if base is None:
            u_ref, c_ref, o_ref = refs
        else:
            u_ref, c_ref, b_ref, o_ref = refs
        c = c_ref[0]
        face_x = c * pltpu.roll(c, rows - 1, 0)
        face_y = c * pltpu.roll(c, columns - 1, 1)

        def step(index, u):
            flux_x = face_x * (pltpu.roll(u, rows - 1, 0) - u)
            change_x = flux_x - pltpu.roll(flux_x, 1, 0)
            flux_y = face_y * (pltpu.roll(u, columns - 1, 1) - u)
            change_y = flux_y - pltpu.roll(flux_y, 1, 1)
            return u + change_x + change_y

        u = lax.fori_loop(0, steps, step, u_ref[0], unroll=True)
        kept = u[:core_rows, :core_columns]
        if base is None:
            o_ref[0] = kept
        else:
            o_ref[0] = b_ref[0] + kept

    in_specs = [
        pl.BlockSpec((1, rows, columns), lambda p: (p + first, 0, 0)),
        pl.BlockSpec((1, rows, columns), coef_plane),
    ]
    operands = [ext, coef]
    if base is not None:
        in_specs.append(pl.BlockSpec((1, core_rows, core_columns), lambda p: (p, 0, 0)))
        operands.append(base)
    return pl.pallas_call(
        kernel,
        grid=(planes,),
        in_specs=in_specs,
        out_specs=pl.BlockSpec((1, core_rows, core_columns), lambda p: (p, 0, 0)),
        out_shape=jax.ShapeDtypeStruct((planes, core_rows, core_columns), jnp.float32),
    )(*operands)


def on_device(
    control, perturb, weights, kappa, wet_levels, obs_index, obs_count, innov, obs_weight
):
    planes, cells_x, cells_y = control.shape
    members = weights.shape[0]
    levels = (planes - 1) // 2
    core = (cells_x, cells_y)
    stack = jnp.concatenate(
        [control, weights, kappa, wet_levels.astype(jnp.float32)[None]], axis=0
    )
    ext = extended(stack, HALO)
    first_kappa = planes + members
    kappa_ext = ext[first_kappa : first_kappa + 4]
    wet_ext = ext[first_kappa + 4]
    level_iota = lax.broadcasted_iota(jnp.int32, (levels, 1, 1), 0).astype(jnp.float32)
    wet_mask = (level_iota < wet_ext[None]).astype(jnp.float32)
    surface = wet_mask[0:1]
    coef = jnp.concatenate(
        [kappa_ext[0:1] * wet_mask, kappa_ext[1:2] * wet_mask, kappa_ext[2:3] * surface, kappa_ext[3:4] * surface],
        axis=0,
    )
    static_plane = lambda p: (p, 0, 0)
    local_plane = lambda p: (planes, 0, 0)
    member_scale = 1.0 / math.sqrt(members * lax.axis_size("ma"))
    static = diffuse_call(ext, 0, coef, static_plane, NSTEP, planes, core)
    local = diffuse_call(ext, planes, coef, local_plane, LSTEP, members, core)
    partial_sum = member_scale * jnp.sum(perturb.astype(jnp.float32) * local[:, None], axis=0)
    ensemble_seen = lax.psum(partial_sum.reshape(-1)[obs_index], "ma")
    static_seen = static.reshape(-1)[obs_index]
    observed = static_seen + ensemble_seen
    live_obs = lax.broadcasted_iota(jnp.int32, obs_index.shape, 0) < obs_count[0]
    misfit = obs_weight * (observed - innov)
    resid = jnp.where(live_obs, misfit, jnp.zeros_like(misfit))
    adjoint = jnp.zeros((planes * cells_x * cells_y,), jnp.float32).at[obs_index].add(resid)
    adjoint = adjoint.reshape(planes, cells_x, cells_y)
    project = member_scale * jnp.sum(perturb.astype(jnp.float32) * adjoint[None], axis=1)
    ext2 = extended(jnp.concatenate([adjoint, project], axis=0), HALO)
    grad_control = diffuse_call(ext2, 0, coef, static_plane, NSTEP, planes, core, base=control)
    grad_weights = diffuse_call(ext2, planes, coef, local_plane, LSTEP, members, core, base=weights)
    return (grad_control, grad_weights)


def solution(mesh):
    placed = (
        P(None, "gx", "gy"),
        P("ma", None, "gx", "gy"),
        P("ma", "gx", "gy"),
        P(None, "gx", "gy"),
        P("gx", "gy"),
        P(("gx", "gy")),
        P(("gx", "gy")),
        P(("gx", "gy")),
        P(("gx", "gy")),
    )
    return jax.shard_map(
        on_device,
        mesh=mesh,
        in_specs=placed,
        out_specs=(P(None, "gx", "gy"), P("ma", "gx", "gy")),
        check_vma=False,
    )
```

```python
import math

import jax
import jax.numpy as jnp
from jax import lax
from jax.experimental import pallas as pl
from jax.experimental.pallas import tpu as pltpu
from jax.sharding import PartitionSpec as P

NSTEP = 10
LSTEP = 4
HALO = NSTEP


def passed_along(value, axis, steps):
    count = lax.axis_size(axis)
    pairs = [(source, (source + steps) % count) for source in range(count)]
    return lax.ppermute(value, axis, pairs)


def shifted(value, axis, steps):
    count = lax.axis_size(axis)
    initial, last = (max(0, -steps), min(count, count - steps))
    return lax.ppermute(value, axis, [(source, source + steps) for source in range(initial, last)])


def round_up(value, unit):
    return (value + unit - 1) // unit * unit


def extended(field, halo):
    planes, rows, columns = field.shape
    total_rows = round_up(rows + 2 * halo, 8)
    total_columns = round_up(columns + 2 * halo, 128)
    east = passed_along(field[:, :halo, :], "gx", -1)
    west = passed_along(field[:, rows - halo :, :], "gx", 1)
    gap = jnp.zeros((planes, total_rows - rows - 2 * halo, columns), field.dtype)
    wide = jnp.concatenate([field, east, gap, west], axis=1)
    north = shifted(wide[:, :, :halo], "gy", -1)
    south = shifted(wide[:, :, columns - halo :], "gy", 1)
    gap = jnp.zeros((planes, total_rows, total_columns - columns - 2 * halo), field.dtype)
    return jnp.concatenate([wide, north, gap, south], axis=2)


def diffuse_call(ext, first, coef, coef_plane, steps, planes, core, base=None):
    _, rows, columns = ext.shape
    core_rows, core_columns = core

    def kernel(*refs):
        if base is None:
            u_ref, c_ref, o_ref = refs
        else:
            u_ref, c_ref, b_ref, o_ref = refs
        c = c_ref[0]
        face_x = c * pltpu.roll(c, rows - 1, 0)
        face_y = c * pltpu.roll(c, columns - 1, 1)

        def step(index, u):
            flux_x = face_x * (pltpu.roll(u, rows - 1, 0) - u)
            change_x = flux_x - pltpu.roll(flux_x, 1, 0)
            flux_y = face_y * (pltpu.roll(u, columns - 1, 1) - u)
            change_y = flux_y - pltpu.roll(flux_y, 1, 1)
            return u + change_x + change_y

        u = lax.fori_loop(0, steps, step, u_ref[0], unroll=True)
        kept = u[:core_rows, :core_columns]
        if base is None:
            o_ref[0] = kept
        else:
            o_ref[0] = b_ref[0] + kept

    in_specs = [
        pl.BlockSpec((1, rows, columns), lambda p: (p + first, 0, 0)),
        pl.BlockSpec((1, rows, columns), coef_plane),
    ]
    operands = [ext, coef]
    if base is not None:
        in_specs.append(pl.BlockSpec((1, core_rows, core_columns), lambda p: (p, 0, 0)))
        operands.append(base)
    return pl.pallas_call(
        kernel,
        grid=(planes,),
        in_specs=in_specs,
        out_specs=pl.BlockSpec((1, core_rows, core_columns), lambda p: (p, 0, 0)),
        out_shape=jax.ShapeDtypeStruct((planes, core_rows, core_columns), jnp.float32),
    )(*operands)


def exact_product(hot, values, contracting):
    high = values.astype(jnp.bfloat16)
    rest = values - high.astype(jnp.float32)
    middle = rest.astype(jnp.bfloat16)
    low = (rest - middle.astype(jnp.float32)).astype(jnp.bfloat16)
    numbers = (contracting, ((), ()))

    def product(piece):
        return lax.dot_general(hot, piece, numbers, preferred_element_type=jnp.float32)

    return product(high) + product(middle) + product(low)


def on_device(
    control, perturb, weights, kappa, wet_levels, obs_index, obs_count, innov, obs_weight
):
    planes, cells_x, cells_y = control.shape
    members = weights.shape[0]
    levels = (planes - 1) // 2
    core = (cells_x, cells_y)
    stack = jnp.concatenate(
        [control, weights, kappa, wet_levels.astype(jnp.float32)[None]], axis=0
    )
    ext = extended(stack, HALO)
    first_kappa = planes + members
    kappa_ext = ext[first_kappa : first_kappa + 4]
    wet_ext = ext[first_kappa + 4]
    level_iota = lax.broadcasted_iota(jnp.int32, (levels, 1, 1), 0).astype(jnp.float32)
    wet_mask = (level_iota < wet_ext[None]).astype(jnp.float32)
    surface = wet_mask[0:1]
    coef = jnp.concatenate(
        [kappa_ext[0:1] * wet_mask, kappa_ext[1:2] * wet_mask, kappa_ext[2:3] * surface, kappa_ext[3:4] * surface],
        axis=0,
    )
    static_plane = lambda p: (p, 0, 0)
    local_plane = lambda p: (planes, 0, 0)
    member_scale = 1.0 / math.sqrt(members * lax.axis_size("ma"))
    static = diffuse_call(ext, 0, coef, static_plane, NSTEP, planes, core)
    local = diffuse_call(ext, planes, coef, local_plane, LSTEP, members, core)
    partial_sum = member_scale * jnp.sum(perturb.astype(jnp.float32) * local[:, None], axis=0)
    cell_rows = planes * cells_x
    row_of = obs_index // cells_y
    column_of = obs_index % cells_y
    row_hot = (row_of[:, None] == lax.broadcasted_iota(jnp.int32, (1, cell_rows), 1)).astype(jnp.bfloat16)
    column_hot = column_of[:, None] == lax.broadcasted_iota(jnp.int32, (1, cells_y), 1)
    both = jnp.concatenate(
        [static.reshape(cell_rows, cells_y), partial_sum.reshape(cell_rows, cells_y)], axis=1
    )
    picked = exact_product(row_hot, both, ((1,), (0,)))
    static_seen = jnp.sum(jnp.where(column_hot, picked[:, :cells_y], 0.0), axis=1)
    partial_seen = jnp.sum(jnp.where(column_hot, picked[:, cells_y:], 0.0), axis=1)
    ensemble_seen = lax.psum(partial_seen, "ma")
    observed = static_seen + ensemble_seen
    live_obs = lax.broadcasted_iota(jnp.int32, obs_index.shape, 0) < obs_count[0]
    misfit = obs_weight * (observed - innov)
    resid = jnp.where(live_obs, misfit, jnp.zeros_like(misfit))
    placed_resid = jnp.where(column_hot, resid[:, None], 0.0)
    adjoint = exact_product(row_hot, placed_resid, ((0,), (0,)))
    adjoint = adjoint.reshape(planes, cells_x, cells_y)
    project = member_scale * jnp.sum(perturb.astype(jnp.float32) * adjoint[None], axis=1)
    ext2 = extended(jnp.concatenate([adjoint, project], axis=0), HALO)
    grad_control = diffuse_call(ext2, 0, coef, static_plane, NSTEP, planes, core, base=control)
    grad_weights = diffuse_call(ext2, planes, coef, local_plane, LSTEP, members, core, base=weights)
    return (grad_control, grad_weights)


def solution(mesh):
    placed = (
        P(None, "gx", "gy"),
        P("ma", None, "gx", "gy"),
        P("ma", "gx", "gy"),
        P(None, "gx", "gy"),
        P("gx", "gy"),
        P(("gx", "gy")),
        P(("gx", "gy")),
        P(("gx", "gy")),
        P(("gx", "gy")),
    )
    return jax.shard_map(
        on_device,
        mesh=mesh,
        in_specs=placed,
        out_specs=(P(None, "gx", "gy"), P("ma", "gx", "gy")),
        check_vma=False,
    )
```

```python
import math

import jax
import jax.numpy as jnp
from jax import lax
from jax.experimental import pallas as pl
from jax.experimental.pallas import tpu as pltpu
from jax.sharding import PartitionSpec as P

NSTEP = 10
LSTEP = 4
HALO = NSTEP


def passed_along(value, axis, steps):
    count = lax.axis_size(axis)
    pairs = [(source, (source + steps) % count) for source in range(count)]
    return lax.ppermute(value, axis, pairs)


def shifted(value, axis, steps):
    count = lax.axis_size(axis)
    initial, last = (max(0, -steps), min(count, count - steps))
    return lax.ppermute(value, axis, [(source, source + steps) for source in range(initial, last)])


def round_up(value, unit):
    return (value + unit - 1) // unit * unit


def extended(field, halo):
    planes, rows, columns = field.shape
    total_rows = round_up(rows + 2 * halo, 8)
    total_columns = round_up(columns + 2 * halo, 128)
    east = passed_along(field[:, :, :halo], "gx", -1)
    west = passed_along(field[:, :, columns - halo :], "gx", 1)
    gap = jnp.zeros((planes, rows, total_columns - columns - 2 * halo), field.dtype)
    wide = jnp.concatenate([field, east, gap, west], axis=2)
    north = shifted(wide[:, :halo], "gy", -1)
    south = shifted(wide[:, rows - halo :], "gy", 1)
    gap = jnp.zeros((planes, total_rows - rows - 2 * halo, total_columns), field.dtype)
    return jnp.concatenate([wide, north, gap, south], axis=1)


def diffuse_call(ext, first, coef, coef_plane, steps, planes, core, base=None):
    _, rows, columns = ext.shape
    core_rows, core_columns = core
    square = 128

    def kernel(*refs):
        if base is None:
            u_ref, c_ref, o_ref = refs
        else:
            u_ref, c_ref, b_ref, o_ref = refs
        c = c_ref[0]
        face_y = c * pltpu.roll(c, rows - 1, 0)
        face_x = c * pltpu.roll(c, columns - 1, 1)

        def step(index, u):
            flux_x = face_x * (pltpu.roll(u, columns - 1, 1) - u)
            change_x = flux_x - pltpu.roll(flux_x, 1, 1)
            flux_y = face_y * (pltpu.roll(u, rows - 1, 0) - u)
            change_y = flux_y - pltpu.roll(flux_y, 1, 0)
            return u + change_x + change_y

        u = lax.fori_loop(0, steps, step, u_ref[0], unroll=True)
        kept = u[:square, :square].T[:core_rows, :core_columns]
        if base is None:
            o_ref[0] = kept
        else:
            o_ref[0] = b_ref[0] + kept

    in_specs = [
        pl.BlockSpec((1, rows, columns), lambda p: (p + first, 0, 0)),
        pl.BlockSpec((1, rows, columns), coef_plane),
    ]
    operands = [ext, coef]
    if base is not None:
        in_specs.append(pl.BlockSpec((1, core_rows, core_columns), lambda p: (p, 0, 0)))
        operands.append(base)
    return pl.pallas_call(
        kernel,
        grid=(planes,),
        in_specs=in_specs,
        out_specs=pl.BlockSpec((1, core_rows, core_columns), lambda p: (p, 0, 0)),
        out_shape=jax.ShapeDtypeStruct((planes, core_rows, core_columns), jnp.float32),
    )(*operands)


def exact_product(hot, values, contracting):
    high = values.astype(jnp.bfloat16)
    rest = values - high.astype(jnp.float32)
    middle = rest.astype(jnp.bfloat16)
    low = (rest - middle.astype(jnp.float32)).astype(jnp.bfloat16)
    width = values.shape[1]
    pieces = jnp.concatenate([high, middle, low], axis=1)
    numbers = (contracting, ((), ()))
    picked = lax.dot_general(hot, pieces, numbers, preferred_element_type=jnp.float32)
    return (picked[:, :width] + picked[:, width : 2 * width]) + picked[:, 2 * width :]


def on_device(
    control, perturb, weights, kappa, wet_levels, obs_index, obs_count, innov, obs_weight
):
    planes, cells_x, cells_y = control.shape
    members = weights.shape[0]
    levels = (planes - 1) // 2
    core = (cells_x, cells_y)
    stack = jnp.concatenate(
        [control, weights, kappa, wet_levels.astype(jnp.float32)[None]], axis=0
    )
    ext = extended(jnp.swapaxes(stack, 1, 2), HALO)
    first_kappa = planes + members
    kappa_ext = ext[first_kappa : first_kappa + 4]
    wet_ext = ext[first_kappa + 4]
    level_iota = lax.broadcasted_iota(jnp.int32, (levels, 1, 1), 0).astype(jnp.float32)
    wet_mask = (level_iota < wet_ext[None]).astype(jnp.float32)
    surface = wet_mask[0:1]
    coef = jnp.concatenate(
        [kappa_ext[0:1] * wet_mask, kappa_ext[1:2] * wet_mask, kappa_ext[2:3] * surface, kappa_ext[3:4] * surface],
        axis=0,
    )
    static_plane = lambda p: (p, 0, 0)
    local_plane = lambda p: (planes, 0, 0)
    member_scale = 1.0 / math.sqrt(members * lax.axis_size("ma"))
    static = diffuse_call(ext, 0, coef, static_plane, NSTEP, planes, core)
    local = diffuse_call(ext, planes, coef, local_plane, LSTEP, members, core)
    partial_sum = member_scale * jnp.sum(perturb.astype(jnp.float32) * local[:, None], axis=0)
    cell_rows = planes * cells_x
    row_of = obs_index // cells_y
    column_of = obs_index % cells_y
    row_hot = (row_of[:, None] == lax.broadcasted_iota(jnp.int32, (1, cell_rows), 1)).astype(jnp.bfloat16)
    column_hot = column_of[:, None] == lax.broadcasted_iota(jnp.int32, (1, cells_y), 1)
    both = jnp.concatenate(
        [static.reshape(cell_rows, cells_y), partial_sum.reshape(cell_rows, cells_y)], axis=1
    )
    picked = exact_product(row_hot, both, ((1,), (0,)))
    static_seen = jnp.sum(jnp.where(column_hot, picked[:, :cells_y], 0.0), axis=1)
    partial_seen = jnp.sum(jnp.where(column_hot, picked[:, cells_y:], 0.0), axis=1)
    ensemble_seen = lax.psum(partial_seen, "ma")
    observed = static_seen + ensemble_seen
    live_obs = lax.broadcasted_iota(jnp.int32, obs_index.shape, 0) < obs_count[0]
    misfit = obs_weight * (observed - innov)
    resid = jnp.where(live_obs, misfit, jnp.zeros_like(misfit))
    placed_resid = jnp.where(column_hot, resid[:, None], 0.0)
    adjoint = exact_product(row_hot, placed_resid, ((0,), (0,)))
    adjoint = adjoint.reshape(planes, cells_x, cells_y)
    project = member_scale * jnp.sum(perturb.astype(jnp.float32) * adjoint[None], axis=1)
    ext2 = extended(jnp.swapaxes(jnp.concatenate([adjoint, project], axis=0), 1, 2), HALO)
    grad_control = diffuse_call(ext2, 0, coef, static_plane, NSTEP, planes, core, base=control)
    grad_weights = diffuse_call(ext2, planes, coef, local_plane, LSTEP, members, core, base=weights)
    return (grad_control, grad_weights)


def solution(mesh):
    placed = (
        P(None, "gx", "gy"),
        P("ma", None, "gx", "gy"),
        P("ma", "gx", "gy"),
        P(None, "gx", "gy"),
        P("gx", "gy"),
        P(("gx", "gy")),
        P(("gx", "gy")),
        P(("gx", "gy")),
        P(("gx", "gy")),
    )
    return jax.shard_map(
        on_device,
        mesh=mesh,
        in_specs=placed,
        out_specs=(P(None, "gx", "gy"), P("ma", "gx", "gy")),
        check_vma=False,
    )
```

```python
import math

import jax
import jax.numpy as jnp
from jax import lax
from jax.experimental import pallas as pl
from jax.experimental.pallas import tpu as pltpu
from jax.sharding import PartitionSpec as P

NSTEP = 10
LSTEP = 4
HALO = NSTEP


def passed_along(value, axis, steps):
    count = lax.axis_size(axis)
    pairs = [(source, (source + steps) % count) for source in range(count)]
    return lax.ppermute(value, axis, pairs)


def shifted(value, axis, steps):
    count = lax.axis_size(axis)
    initial, last = (max(0, -steps), min(count, count - steps))
    return lax.ppermute(value, axis, [(source, source + steps) for source in range(initial, last)])


def round_up(value, unit):
    return (value + unit - 1) // unit * unit


def extended(field, halo):
    planes, rows, columns = field.shape
    total_rows = round_up(rows + 2 * halo, 8)
    total_columns = round_up(columns + 2 * halo, 128)
    east = passed_along(field[:, :halo, :], "gx", -1)
    west = passed_along(field[:, rows - halo :, :], "gx", 1)
    gap = jnp.zeros((planes, total_rows - rows - 2 * halo, columns), field.dtype)
    wide = jnp.concatenate([field, east, gap, west], axis=1)
    north = shifted(wide[:, :, :halo], "gy", -1)
    south = shifted(wide[:, :, columns - halo :], "gy", 1)
    gap = jnp.zeros((planes, total_rows, total_columns - columns - 2 * halo), field.dtype)
    return jnp.concatenate([wide, north, gap, south], axis=2)


def diffuse_call(ext, first, coef, coef_plane, steps, planes, core, base=None):
    _, rows, columns = ext.shape
    core_rows, core_columns = core

    def kernel(*refs):
        if base is None:
            u_ref, c_ref, o_ref = refs
        else:
            u_ref, c_ref, b_ref, o_ref = refs
        c = c_ref[0]
        face_x = c * pltpu.roll(c, rows - 1, 0)
        face_y = c * pltpu.roll(c, columns - 1, 1)

        def step(index, u):
            flux_x = face_x * (pltpu.roll(u, rows - 1, 0) - u)
            change_x = flux_x - pltpu.roll(flux_x, 1, 0)
            flux_y = face_y * (pltpu.roll(u, columns - 1, 1) - u)
            change_y = flux_y - pltpu.roll(flux_y, 1, 1)
            return u + change_x + change_y

        u = lax.fori_loop(0, steps, step, u_ref[0], unroll=True)
        kept = u[:core_rows, :core_columns]
        if base is None:
            o_ref[0] = kept
        else:
            o_ref[0] = b_ref[0] + kept

    in_specs = [
        pl.BlockSpec((1, rows, columns), lambda p: (p + first, 0, 0)),
        pl.BlockSpec((1, rows, columns), coef_plane),
    ]
    operands = [ext, coef]
    if base is not None:
        in_specs.append(pl.BlockSpec((1, core_rows, core_columns), lambda p: (p, 0, 0)))
        operands.append(base)
    return pl.pallas_call(
        kernel,
        grid=(planes,),
        in_specs=in_specs,
        out_specs=pl.BlockSpec((1, core_rows, core_columns), lambda p: (p, 0, 0)),
        out_shape=jax.ShapeDtypeStruct((planes, core_rows, core_columns), jnp.float32),
    )(*operands)


def exact_product(hot, values, contracting):
    high = values.astype(jnp.bfloat16)
    rest = values - high.astype(jnp.float32)
    middle = rest.astype(jnp.bfloat16)
    low = (rest - middle.astype(jnp.float32)).astype(jnp.bfloat16)
    width = values.shape[1]
    pieces = jnp.concatenate([high, middle, low], axis=1)
    numbers = (contracting, ((), ()))
    picked = lax.dot_general(hot, pieces, numbers, preferred_element_type=jnp.float32)
    return (picked[:, :width] + picked[:, width : 2 * width]) + picked[:, 2 * width :]


def on_device(
    control, perturb, weights, kappa, wet_levels, obs_index, obs_count, innov, obs_weight
):
    planes, cells_x, cells_y = control.shape
    members = weights.shape[0]
    levels = (planes - 1) // 2
    core = (cells_x, cells_y)
    stack = jnp.concatenate(
        [control, weights, kappa, wet_levels.astype(jnp.float32)[None]], axis=0
    )
    ext = extended(stack, HALO)
    first_kappa = planes + members
    kappa_ext = ext[first_kappa : first_kappa + 4]
    wet_ext = ext[first_kappa + 4]
    level_iota = lax.broadcasted_iota(jnp.int32, (levels, 1, 1), 0).astype(jnp.float32)
    wet_mask = (level_iota < wet_ext[None]).astype(jnp.float32)
    surface = wet_mask[0:1]
    coef = jnp.concatenate(
        [kappa_ext[0:1] * wet_mask, kappa_ext[1:2] * wet_mask, kappa_ext[2:3] * surface, kappa_ext[3:4] * surface],
        axis=0,
    )
    static_plane = lambda p: (p, 0, 0)
    local_plane = lambda p: (planes, 0, 0)
    member_scale = 1.0 / math.sqrt(members * lax.axis_size("ma"))
    static = diffuse_call(ext, 0, coef, static_plane, NSTEP, planes, core)
    local = diffuse_call(ext, planes, coef, local_plane, LSTEP, members, core)
    partial_sum = member_scale * jnp.sum(perturb.astype(jnp.float32) * local[:, None], axis=0)
    cell_rows = planes * cells_x
    row_of = obs_index // cells_y
    column_of = obs_index % cells_y
    row_hot = (row_of[:, None] == lax.broadcasted_iota(jnp.int32, (1, cell_rows), 1)).astype(jnp.bfloat16)
    column_hot = column_of[:, None] == lax.broadcasted_iota(jnp.int32, (1, cells_y), 1)
    both = jnp.concatenate(
        [static.reshape(cell_rows, cells_y), partial_sum.reshape(cell_rows, cells_y)], axis=1
    )
    picked = exact_product(row_hot, both, ((1,), (0,)))
    static_seen = jnp.sum(jnp.where(column_hot, picked[:, :cells_y], 0.0), axis=1)
    partial_seen = jnp.sum(jnp.where(column_hot, picked[:, cells_y:], 0.0), axis=1)
    ensemble_seen = lax.psum(partial_seen, "ma")
    observed = static_seen + ensemble_seen
    live_obs = lax.broadcasted_iota(jnp.int32, obs_index.shape, 0) < obs_count[0]
    misfit = obs_weight * (observed - innov)
    resid = jnp.where(live_obs, misfit, jnp.zeros_like(misfit))
    placed_resid = jnp.where(column_hot, resid[:, None], 0.0)
    adjoint = exact_product(row_hot, placed_resid, ((0,), (0,)))
    adjoint = adjoint.reshape(planes, cells_x, cells_y)
    project = member_scale * jnp.sum(perturb.astype(jnp.float32) * adjoint[None], axis=1)
    ext2 = extended(jnp.concatenate([adjoint, project], axis=0), HALO)
    grad_control = diffuse_call(ext2, 0, coef, static_plane, NSTEP, planes, core, base=control)
    grad_weights = diffuse_call(ext2, planes, coef, local_plane, LSTEP, members, core, base=weights)
    return (grad_control, grad_weights)


def solution(mesh):
    placed = (
        P(None, "gx", "gy"),
        P("ma", None, "gx", "gy"),
        P("ma", "gx", "gy"),
        P(None, "gx", "gy"),
        P("gx", "gy"),
        P(("gx", "gy")),
        P(("gx", "gy")),
        P(("gx", "gy")),
        P(("gx", "gy")),
    )
    return jax.shard_map(
        on_device,
        mesh=mesh,
        in_specs=placed,
        out_specs=(P(None, "gx", "gy"), P("ma", "gx", "gy")),
        check_vma=False,
    )
```

```python
import math

import jax
import jax.numpy as jnp
from jax import lax
from jax.experimental import pallas as pl
from jax.experimental.pallas import tpu as pltpu
from jax.sharding import PartitionSpec as P

NSTEP = 10
LSTEP = 4
HALO = NSTEP


def passed_along(value, axis, steps):
    count = lax.axis_size(axis)
    pairs = [(source, (source + steps) % count) for source in range(count)]
    return lax.ppermute(value, axis, pairs)


def shifted(value, axis, steps):
    count = lax.axis_size(axis)
    initial, last = (max(0, -steps), min(count, count - steps))
    return lax.ppermute(value, axis, [(source, source + steps) for source in range(initial, last)])


def round_up(value, unit):
    return (value + unit - 1) // unit * unit


def extended(field, halo):
    planes, rows, columns = field.shape
    total_rows = round_up(rows + 2 * halo, 8)
    total_columns = round_up(columns + 2 * halo, 128)
    east = passed_along(field[:, :halo, :], "gx", -1)
    west = passed_along(field[:, rows - halo :, :], "gx", 1)
    gap = jnp.zeros((planes, total_rows - rows - 2 * halo, columns), field.dtype)
    wide = jnp.concatenate([field, east, gap, west], axis=1)
    north = shifted(wide[:, :, :halo], "gy", -1)
    south = shifted(wide[:, :, columns - halo :], "gy", 1)
    gap = jnp.zeros((planes, total_rows, total_columns - columns - 2 * halo), field.dtype)
    return jnp.concatenate([wide, north, gap, south], axis=2)


def diffuse_call(ext, first, coef, coef_plane, steps, planes, core, offset, count, base=None):
    _, rows, columns = ext.shape
    core_rows, core_columns = core

    def kernel(offset_ref, *refs):
        if base is None:
            u_ref, c_ref, o_ref = refs
        else:
            u_ref, c_ref, b_ref, o_ref = refs
        c = c_ref[0]
        face_x = c * pltpu.roll(c, rows - 1, 0)
        face_y = c * pltpu.roll(c, columns - 1, 1)

        def step(index, u):
            flux_x = face_x * (pltpu.roll(u, rows - 1, 0) - u)
            change_x = flux_x - pltpu.roll(flux_x, 1, 0)
            flux_y = face_y * (pltpu.roll(u, columns - 1, 1) - u)
            change_y = flux_y - pltpu.roll(flux_y, 1, 1)
            return u + change_x + change_y

        u = lax.fori_loop(0, steps, step, u_ref[0], unroll=True)
        kept = u[:core_rows, :core_columns]
        if base is None:
            o_ref[0] = kept
        else:
            o_ref[0] = b_ref[0] + kept

    def plane(p, offset_ref):
        return jnp.minimum(offset_ref[0] + p, planes - 1)

    in_specs = [
        pl.BlockSpec((1, rows, columns), lambda p, o: (plane(p, o) + first, 0, 0)),
        pl.BlockSpec((1, rows, columns), lambda p, o: (coef_plane(plane(p, o)), 0, 0)),
    ]
    operands = [ext, coef]
    if base is not None:
        in_specs.append(pl.BlockSpec((1, core_rows, core_columns), lambda p, o: (plane(p, o), 0, 0)))
        operands.append(base)
    grid_spec = pltpu.PrefetchScalarGridSpec(
        num_scalar_prefetch=1,
        grid=(count,),
        in_specs=in_specs,
        out_specs=pl.BlockSpec((1, core_rows, core_columns), lambda p, o: (p, 0, 0)),
    )
    return pl.pallas_call(
        kernel,
        grid_spec=grid_spec,
        out_shape=jax.ShapeDtypeStruct((count, core_rows, core_columns), jnp.float32),
    )(offset, *operands)


def exact_product(hot, values, contracting):
    high = values.astype(jnp.bfloat16)
    rest = values - high.astype(jnp.float32)
    middle = rest.astype(jnp.bfloat16)
    low = (rest - middle.astype(jnp.float32)).astype(jnp.bfloat16)
    width = values.shape[1]
    pieces = jnp.concatenate([high, middle, low], axis=1)
    numbers = (contracting, ((), ()))
    picked = lax.dot_general(hot, pieces, numbers, preferred_element_type=jnp.float32)
    return (picked[:, :width] + picked[:, width : 2 * width]) + picked[:, 2 * width :]


def on_device(
    control, perturb, weights, kappa, wet_levels, obs_index, obs_count, innov, obs_weight
):
    planes, cells_x, cells_y = control.shape
    members = weights.shape[0]
    levels = (planes - 1) // 2
    core = (cells_x, cells_y)
    stack = jnp.concatenate(
        [control, weights, kappa, wet_levels.astype(jnp.float32)[None]], axis=0
    )
    ext = extended(stack, HALO)
    first_kappa = planes + members
    kappa_ext = ext[first_kappa : first_kappa + 4]
    wet_ext = ext[first_kappa + 4]
    level_iota = lax.broadcasted_iota(jnp.int32, (levels, 1, 1), 0).astype(jnp.float32)
    wet_mask = (level_iota < wet_ext[None]).astype(jnp.float32)
    surface = wet_mask[0:1]
    coef = jnp.concatenate(
        [kappa_ext[0:1] * wet_mask, kappa_ext[1:2] * wet_mask, kappa_ext[2:3] * surface, kappa_ext[3:4] * surface],
        axis=0,
    )
    static_plane = lambda p: p
    local_plane = lambda p: planes
    member_scale = 1.0 / math.sqrt(members * lax.axis_size("ma"))
    share = -(-planes // lax.axis_size("ma"))
    first_plane = lax.axis_index("ma").astype(jnp.int32) * share
    offset = jnp.reshape(first_plane, (1,))
    no_offset = jnp.zeros((1,), jnp.int32)
    static_share = diffuse_call(ext, 0, coef, static_plane, NSTEP, planes, core, offset, share)
    local = diffuse_call(ext, planes, coef, local_plane, LSTEP, members, core, no_offset, members)
    partial_sum = member_scale * jnp.sum(perturb.astype(jnp.float32) * local[:, None], axis=0)
    cell_rows = planes * cells_x
    share_rows = share * cells_x
    row_of = obs_index // cells_y
    column_of = obs_index % cells_y
    row_hot = (row_of[:, None] == lax.broadcasted_iota(jnp.int32, (1, cell_rows), 1)).astype(jnp.bfloat16)
    column_hot = column_of[:, None] == lax.broadcasted_iota(jnp.int32, (1, cells_y), 1)
    share_row = row_of - first_plane * cells_x
    share_row = jnp.where((share_row >= 0) & (share_row < share_rows), share_row, -1)
    share_hot = (share_row[:, None] == lax.broadcasted_iota(jnp.int32, (1, share_rows), 1)).astype(jnp.bfloat16)
    static_picked = exact_product(share_hot, static_share.reshape(share_rows, cells_y), ((1,), (0,)))
    partial_picked = exact_product(row_hot, partial_sum.reshape(cell_rows, cells_y), ((1,), (0,)))
    static_seen = jnp.sum(jnp.where(column_hot, static_picked, 0.0), axis=1)
    partial_seen = jnp.sum(jnp.where(column_hot, partial_picked, 0.0), axis=1)
    observed = lax.psum(static_seen + partial_seen, "ma")
    live_obs = lax.broadcasted_iota(jnp.int32, obs_index.shape, 0) < obs_count[0]
    misfit = obs_weight * (observed - innov)
    resid = jnp.where(live_obs, misfit, jnp.zeros_like(misfit))
    placed_resid = jnp.where(column_hot, resid[:, None], 0.0)
    adjoint = exact_product(row_hot, placed_resid, ((0,), (0,)))
    adjoint = adjoint.reshape(planes, cells_x, cells_y)
    project = member_scale * jnp.sum(perturb.astype(jnp.float32) * adjoint[None], axis=1)
    ext2 = extended(jnp.concatenate([adjoint, project], axis=0), HALO)
    grad_share = diffuse_call(ext2, 0, coef, static_plane, NSTEP, planes, core, offset, share, base=control)
    grad_control = lax.all_gather(grad_share, "ma", axis=0, tiled=True)[:planes]
    grad_weights = diffuse_call(ext2, planes, coef, local_plane, LSTEP, members, core, no_offset, members, base=weights)
    return (grad_control, grad_weights)


def solution(mesh):
    placed = (
        P(None, "gx", "gy"),
        P("ma", None, "gx", "gy"),
        P("ma", "gx", "gy"),
        P(None, "gx", "gy"),
        P("gx", "gy"),
        P(("gx", "gy")),
        P(("gx", "gy")),
        P(("gx", "gy")),
        P(("gx", "gy")),
    )
    return jax.shard_map(
        on_device,
        mesh=mesh,
        in_specs=placed,
        out_specs=(P(None, "gx", "gy"), P("ma", "gx", "gy")),
        check_vma=False,
    )
```

```python
import math

import jax
import jax.numpy as jnp
from jax import lax
from jax.experimental import pallas as pl
from jax.experimental.pallas import tpu as pltpu
from jax.sharding import PartitionSpec as P

NSTEP = 10
LSTEP = 4
HALO = NSTEP


def passed_along(value, axis, steps):
    count = lax.axis_size(axis)
    pairs = [(source, (source + steps) % count) for source in range(count)]
    return lax.ppermute(value, axis, pairs)


def shifted(value, axis, steps):
    count = lax.axis_size(axis)
    initial, last = (max(0, -steps), min(count, count - steps))
    return lax.ppermute(value, axis, [(source, source + steps) for source in range(initial, last)])


def round_up(value, unit):
    return (value + unit - 1) // unit * unit


def extended(field, halo):
    planes, rows, columns = field.shape
    total_rows = round_up(rows + 2 * halo, 8)
    total_columns = round_up(columns + 2 * halo, 128)
    east = passed_along(field[:, :halo, :], "gx", -1)
    west = passed_along(field[:, rows - halo :, :], "gx", 1)
    gap = jnp.zeros((planes, total_rows - rows - 2 * halo, columns), field.dtype)
    wide = jnp.concatenate([field, east, gap, west], axis=1)
    north = shifted(wide[:, :, :halo], "gy", -1)
    south = shifted(wide[:, :, columns - halo :], "gy", 1)
    gap = jnp.zeros((planes, total_rows, total_columns - columns - 2 * halo), field.dtype)
    return jnp.concatenate([wide, north, gap, south], axis=2)


def diffuse_call(ext, first, coef, coef_plane, steps, planes, core, offset, count, base=None):
    _, rows, columns = ext.shape
    core_rows, core_columns = core

    def kernel(offset_ref, *refs):
        if base is None:
            u_ref, c_ref, o_ref = refs
        else:
            u_ref, c_ref, b_ref, o_ref = refs
        c = c_ref[0]
        face_x = c * pltpu.roll(c, rows - 1, 0)
        face_y = c * pltpu.roll(c, columns - 1, 1)

        def step(index, u):
            flux_x = face_x * (pltpu.roll(u, rows - 1, 0) - u)
            change_x = flux_x - pltpu.roll(flux_x, 1, 0)
            flux_y = face_y * (pltpu.roll(u, columns - 1, 1) - u)
            change_y = flux_y - pltpu.roll(flux_y, 1, 1)
            return u + change_x + change_y

        u = lax.fori_loop(0, steps, step, u_ref[0], unroll=True)
        kept = u[:core_rows, :core_columns]
        if base is None:
            o_ref[0] = kept
        else:
            o_ref[0] = b_ref[0] + kept

    def plane(p, offset_ref):
        return jnp.minimum(offset_ref[0] + p, planes - 1)

    in_specs = [
        pl.BlockSpec((1, rows, columns), lambda p, o: (plane(p, o) + first, 0, 0)),
        pl.BlockSpec((1, rows, columns), lambda p, o: (coef_plane(plane(p, o)), 0, 0)),
    ]
    operands = [ext, coef]
    if base is not None:
        in_specs.append(pl.BlockSpec((1, core_rows, core_columns), lambda p, o: (plane(p, o), 0, 0)))
        operands.append(base)
    grid_spec = pltpu.PrefetchScalarGridSpec(
        num_scalar_prefetch=1,
        grid=(count,),
        in_specs=in_specs,
        out_specs=pl.BlockSpec((1, core_rows, core_columns), lambda p, o: (p, 0, 0)),
    )
    return pl.pallas_call(
        kernel,
        grid_spec=grid_spec,
        out_shape=jax.ShapeDtypeStruct((count, core_rows, core_columns), jnp.float32),
    )(offset, *operands)


def exact_product(hot, values, contracting):
    high = values.astype(jnp.bfloat16)
    rest = values - high.astype(jnp.float32)
    middle = rest.astype(jnp.bfloat16)
    low = (rest - middle.astype(jnp.float32)).astype(jnp.bfloat16)
    width = values.shape[1]
    pieces = jnp.concatenate([high, middle, low], axis=1)
    numbers = (contracting, ((), ()))
    picked = lax.dot_general(hot, pieces, numbers, preferred_element_type=jnp.float32)
    return (picked[:, :width] + picked[:, width : 2 * width]) + picked[:, 2 * width :]


def gathered_shares(share):
    count = lax.axis_size("ma")
    here = lax.axis_index("ma").astype(jnp.int32)
    whole = jnp.zeros((count,) + share.shape, share.dtype)
    for steps in range(count):
        if steps == 0:
            piece = share
        else:
            piece = passed_along(share, "ma", steps)
        source = (here - steps) % count
        whole = lax.dynamic_update_index_in_dim(whole, piece, source, 0)
    return whole.reshape((count * share.shape[0],) + share.shape[1:])


def on_device(
    control, perturb, weights, kappa, wet_levels, obs_index, obs_count, innov, obs_weight
):
    planes, cells_x, cells_y = control.shape
    members = weights.shape[0]
    levels = (planes - 1) // 2
    core = (cells_x, cells_y)
    stack = jnp.concatenate(
        [control, weights, kappa, wet_levels.astype(jnp.float32)[None]], axis=0
    )
    ext = extended(stack, HALO)
    first_kappa = planes + members
    kappa_ext = ext[first_kappa : first_kappa + 4]
    wet_ext = ext[first_kappa + 4]
    level_iota = lax.broadcasted_iota(jnp.int32, (levels, 1, 1), 0).astype(jnp.float32)
    wet_mask = (level_iota < wet_ext[None]).astype(jnp.float32)
    surface = wet_mask[0:1]
    coef = jnp.concatenate(
        [kappa_ext[0:1] * wet_mask, kappa_ext[1:2] * wet_mask, kappa_ext[2:3] * surface, kappa_ext[3:4] * surface],
        axis=0,
    )
    static_plane = lambda p: p
    local_plane = lambda p: planes
    member_scale = 1.0 / math.sqrt(members * lax.axis_size("ma"))
    share = -(-planes // lax.axis_size("ma"))
    first_plane = lax.axis_index("ma").astype(jnp.int32) * share
    offset = jnp.reshape(first_plane, (1,))
    no_offset = jnp.zeros((1,), jnp.int32)
    static_share = diffuse_call(ext, 0, coef, static_plane, NSTEP, planes, core, offset, share)
    local = diffuse_call(ext, planes, coef, local_plane, LSTEP, members, core, no_offset, members)
    partial_sum = member_scale * jnp.sum(perturb.astype(jnp.float32) * local[:, None], axis=0)
    cell_rows = planes * cells_x
    share_rows = share * cells_x
    row_of = obs_index // cells_y
    column_of = obs_index % cells_y
    row_hot = (row_of[:, None] == lax.broadcasted_iota(jnp.int32, (1, cell_rows), 1)).astype(jnp.bfloat16)
    column_hot = column_of[:, None] == lax.broadcasted_iota(jnp.int32, (1, cells_y), 1)
    share_row = row_of - first_plane * cells_x
    share_row = jnp.where((share_row >= 0) & (share_row < share_rows), share_row, -1)
    share_hot = (share_row[:, None] == lax.broadcasted_iota(jnp.int32, (1, share_rows), 1)).astype(jnp.bfloat16)
    static_picked = exact_product(share_hot, static_share.reshape(share_rows, cells_y), ((1,), (0,)))
    partial_picked = exact_product(row_hot, partial_sum.reshape(cell_rows, cells_y), ((1,), (0,)))
    static_seen = jnp.sum(jnp.where(column_hot, static_picked, 0.0), axis=1)
    partial_seen = jnp.sum(jnp.where(column_hot, partial_picked, 0.0), axis=1)
    observed = lax.psum(static_seen + partial_seen, "ma")
    live_obs = lax.broadcasted_iota(jnp.int32, obs_index.shape, 0) < obs_count[0]
    misfit = obs_weight * (observed - innov)
    resid = jnp.where(live_obs, misfit, jnp.zeros_like(misfit))
    placed_resid = jnp.where(column_hot, resid[:, None], 0.0)
    adjoint = exact_product(row_hot, placed_resid, ((0,), (0,)))
    adjoint = adjoint.reshape(planes, cells_x, cells_y)
    project = member_scale * jnp.sum(perturb.astype(jnp.float32) * adjoint[None], axis=1)
    ext2 = extended(jnp.concatenate([adjoint, project], axis=0), HALO)
    grad_share = diffuse_call(ext2, 0, coef, static_plane, NSTEP, planes, core, offset, share, base=control)
    grad_control = gathered_shares(grad_share)[:planes]
    grad_weights = diffuse_call(ext2, planes, coef, local_plane, LSTEP, members, core, no_offset, members, base=weights)
    return (grad_control, grad_weights)


def solution(mesh):
    placed = (
        P(None, "gx", "gy"),
        P("ma", None, "gx", "gy"),
        P("ma", "gx", "gy"),
        P(None, "gx", "gy"),
        P("gx", "gy"),
        P(("gx", "gy")),
        P(("gx", "gy")),
        P(("gx", "gy")),
        P(("gx", "gy")),
    )
    return jax.shard_map(
        on_device,
        mesh=mesh,
        in_specs=placed,
        out_specs=(P(None, "gx", "gy"), P("ma", "gx", "gy")),
        check_vma=False,
    )
```

```python
import math

import jax
import jax.numpy as jnp
from jax import lax
from jax.experimental import pallas as pl
from jax.experimental.pallas import tpu as pltpu
from jax.sharding import PartitionSpec as P

NSTEP = 10
LSTEP = 4
HALO = NSTEP


def passed_along(value, axis, steps):
    count = lax.axis_size(axis)
    pairs = [(source, (source + steps) % count) for source in range(count)]
    return lax.ppermute(value, axis, pairs)


def shifted(value, axis, steps):
    count = lax.axis_size(axis)
    initial, last = (max(0, -steps), min(count, count - steps))
    return lax.ppermute(value, axis, [(source, source + steps) for source in range(initial, last)])


def round_up(value, unit):
    return (value + unit - 1) // unit * unit


def extended(field, halo):
    planes, rows, columns = field.shape
    total_rows = round_up(rows + 2 * halo, 8)
    total_columns = round_up(columns + 2 * halo, 128)
    east = passed_along(field[:, :halo, :], "gx", -1)
    west = passed_along(field[:, rows - halo :, :], "gx", 1)
    gap = jnp.zeros((planes, total_rows - rows - 2 * halo, columns), field.dtype)
    wide = jnp.concatenate([field, east, gap, west], axis=1)
    north = shifted(wide[:, :, :halo], "gy", -1)
    south = shifted(wide[:, :, columns - halo :], "gy", 1)
    gap = jnp.zeros((planes, total_rows, total_columns - columns - 2 * halo), field.dtype)
    return jnp.concatenate([wide, north, gap, south], axis=2)


def diffuse_call(ext, first, coef, coef_plane, steps, planes, core, offset, count, base=None):
    _, rows, columns = ext.shape
    core_rows, core_columns = core

    def kernel(offset_ref, *refs):
        if base is None:
            u_ref, c_ref, o_ref = refs
        else:
            u_ref, c_ref, b_ref, o_ref = refs
        c = c_ref[0]
        face_x = c * pltpu.roll(c, rows - 1, 0)
        face_y = c * pltpu.roll(c, columns - 1, 1)

        def step(index, u):
            flux_x = face_x * (pltpu.roll(u, rows - 1, 0) - u)
            change_x = flux_x - pltpu.roll(flux_x, 1, 0)
            flux_y = face_y * (pltpu.roll(u, columns - 1, 1) - u)
            change_y = flux_y - pltpu.roll(flux_y, 1, 1)
            return u + change_x + change_y

        u = lax.fori_loop(0, steps, step, u_ref[0], unroll=True)
        kept = u[:core_rows, :core_columns]
        if base is None:
            o_ref[0] = kept
        else:
            o_ref[0] = b_ref[0] + kept

    def plane(p, offset_ref):
        return jnp.minimum(offset_ref[0] + p, planes - 1)

    in_specs = [
        pl.BlockSpec((1, rows, columns), lambda p, o: (p + first, 0, 0)),
        pl.BlockSpec((1, rows, columns), lambda p, o: (coef_plane(plane(p, o)), 0, 0)),
    ]
    operands = [ext, coef]
    if base is not None:
        in_specs.append(pl.BlockSpec((1, core_rows, core_columns), lambda p, o: (plane(p, o), 0, 0)))
        operands.append(base)
    grid_spec = pltpu.PrefetchScalarGridSpec(
        num_scalar_prefetch=1,
        grid=(count,),
        in_specs=in_specs,
        out_specs=pl.BlockSpec((1, core_rows, core_columns), lambda p, o: (p, 0, 0)),
    )
    return pl.pallas_call(
        kernel,
        grid_spec=grid_spec,
        out_shape=jax.ShapeDtypeStruct((count, core_rows, core_columns), jnp.float32),
    )(offset, *operands)


def exact_product(hot, values, contracting):
    high = values.astype(jnp.bfloat16)
    rest = values - high.astype(jnp.float32)
    middle = rest.astype(jnp.bfloat16)
    low = (rest - middle.astype(jnp.float32)).astype(jnp.bfloat16)
    width = values.shape[1]
    pieces = jnp.concatenate([high, middle, low], axis=1)
    numbers = (contracting, ((), ()))
    picked = lax.dot_general(hot, pieces, numbers, preferred_element_type=jnp.float32)
    return (picked[:, :width] + picked[:, width : 2 * width]) + picked[:, 2 * width :]


def gathered_shares(share, total):
    count = lax.axis_size("ma")
    here = lax.axis_index("ma").astype(jnp.int32)
    whole = jnp.zeros((count,) + share.shape, share.dtype)
    for steps in range(count):
        if steps == 0:
            piece = share
        else:
            piece = passed_along(share, "ma", steps)
        source = (here - steps) % count
        whole = lax.dynamic_update_index_in_dim(whole, piece, source, 0)
    head = whole[: count - 1].reshape(((count - 1) * share.shape[0],) + share.shape[1:])
    return jnp.concatenate([head, whole[count - 1, count * share.shape[0] - total :]], axis=0)


def on_device(
    control, perturb, weights, kappa, wet_levels, obs_index, obs_count, innov, obs_weight
):
    planes, cells_x, cells_y = control.shape
    members = weights.shape[0]
    levels = (planes - 1) // 2
    core = (cells_x, cells_y)
    share = -(-planes // lax.axis_size("ma"))
    nominal_first = lax.axis_index("ma").astype(jnp.int32) * share
    first_plane = jnp.minimum(nominal_first, planes - share)
    offset = jnp.reshape(first_plane, (1,))
    no_offset = jnp.zeros((1,), jnp.int32)
    control_share = lax.dynamic_slice_in_dim(control, first_plane, share, 0)
    stack = jnp.concatenate(
        [control_share, weights, kappa, wet_levels.astype(jnp.float32)[None]], axis=0
    )
    ext = extended(stack, HALO)
    first_kappa = share + members
    kappa_ext = ext[first_kappa : first_kappa + 4]
    wet_ext = ext[first_kappa + 4]
    level_iota = lax.broadcasted_iota(jnp.int32, (levels, 1, 1), 0).astype(jnp.float32)
    wet_mask = (level_iota < wet_ext[None]).astype(jnp.float32)
    surface = wet_mask[0:1]
    coef = jnp.concatenate(
        [kappa_ext[0:1] * wet_mask, kappa_ext[1:2] * wet_mask, kappa_ext[2:3] * surface, kappa_ext[3:4] * surface],
        axis=0,
    )
    static_plane = lambda p: p
    local_plane = lambda p: planes
    member_scale = 1.0 / math.sqrt(members * lax.axis_size("ma"))
    static_share = diffuse_call(ext, 0, coef, static_plane, NSTEP, planes, core, offset, share)
    local = diffuse_call(ext, share, coef, local_plane, LSTEP, members, core, no_offset, members)
    partial_sum = member_scale * jnp.sum(perturb.astype(jnp.float32) * local[:, None], axis=0)
    cell_rows = planes * cells_x
    share_rows = share * cells_x
    row_of = obs_index // cells_y
    column_of = obs_index % cells_y
    row_hot = (row_of[:, None] == lax.broadcasted_iota(jnp.int32, (1, cell_rows), 1)).astype(jnp.bfloat16)
    column_hot = column_of[:, None] == lax.broadcasted_iota(jnp.int32, (1, cells_y), 1)
    plane_of = row_of // cells_x
    owned = (plane_of >= nominal_first) & (plane_of < nominal_first + share)
    share_row = jnp.where(owned, row_of - first_plane * cells_x, -1)
    share_hot = (share_row[:, None] == lax.broadcasted_iota(jnp.int32, (1, share_rows), 1)).astype(jnp.bfloat16)
    static_picked = exact_product(share_hot, static_share.reshape(share_rows, cells_y), ((1,), (0,)))
    partial_picked = exact_product(row_hot, partial_sum.reshape(cell_rows, cells_y), ((1,), (0,)))
    static_seen = jnp.sum(jnp.where(column_hot, static_picked, 0.0), axis=1)
    partial_seen = jnp.sum(jnp.where(column_hot, partial_picked, 0.0), axis=1)
    observed = lax.psum(static_seen + partial_seen, "ma")
    live_obs = lax.broadcasted_iota(jnp.int32, obs_index.shape, 0) < obs_count[0]
    misfit = obs_weight * (observed - innov)
    resid = jnp.where(live_obs, misfit, jnp.zeros_like(misfit))
    placed_resid = jnp.where(column_hot, resid[:, None], 0.0)
    adjoint = exact_product(row_hot, placed_resid, ((0,), (0,)))
    adjoint = adjoint.reshape(planes, cells_x, cells_y)
    project = member_scale * jnp.sum(perturb.astype(jnp.float32) * adjoint[None], axis=1)
    adjoint_share = lax.dynamic_slice_in_dim(adjoint, first_plane, share, 0)
    ext2 = extended(jnp.concatenate([adjoint_share, project], axis=0), HALO)
    grad_share = diffuse_call(ext2, 0, coef, static_plane, NSTEP, planes, core, offset, share, base=control)
    grad_control = gathered_shares(grad_share, planes)
    grad_weights = diffuse_call(ext2, share, coef, local_plane, LSTEP, members, core, no_offset, members, base=weights)
    return (grad_control, grad_weights)


def solution(mesh):
    placed = (
        P(None, "gx", "gy"),
        P("ma", None, "gx", "gy"),
        P("ma", "gx", "gy"),
        P(None, "gx", "gy"),
        P("gx", "gy"),
        P(("gx", "gy")),
        P(("gx", "gy")),
        P(("gx", "gy")),
        P(("gx", "gy")),
    )
    return jax.shard_map(
        on_device,
        mesh=mesh,
        in_specs=placed,
        out_specs=(P(None, "gx", "gy"), P("ma", "gx", "gy")),
        check_vma=False,
    )
```

```python
import math

import jax
import jax.numpy as jnp
from jax import lax
from jax.experimental import pallas as pl
from jax.experimental.pallas import tpu as pltpu
from jax.sharding import PartitionSpec as P

NSTEP = 10
LSTEP = 4
HALO = NSTEP


def passed_along(value, axis, steps):
    count = lax.axis_size(axis)
    pairs = [(source, (source + steps) % count) for source in range(count)]
    return lax.ppermute(value, axis, pairs)


def shifted(value, axis, steps):
    count = lax.axis_size(axis)
    initial, last = (max(0, -steps), min(count, count - steps))
    return lax.ppermute(value, axis, [(source, source + steps) for source in range(initial, last)])


def round_up(value, unit):
    return (value + unit - 1) // unit * unit


def extended(field, halo):
    planes, rows, columns = field.shape
    total_rows = round_up(rows + 2 * halo, 8)
    total_columns = round_up(columns + 2 * halo, 128)
    east = passed_along(field[:, :halo, :], "gx", -1)
    west = passed_along(field[:, rows - halo :, :], "gx", 1)
    gap = jnp.zeros((planes, total_rows - rows - 2 * halo, columns), field.dtype)
    wide = jnp.concatenate([field, east, gap, west], axis=1)
    north = shifted(wide[:, :, :halo], "gy", -1)
    south = shifted(wide[:, :, columns - halo :], "gy", 1)
    gap = jnp.zeros((planes, total_rows, total_columns - columns - 2 * halo), field.dtype)
    return jnp.concatenate([wide, north, gap, south], axis=2)


def diffuse_call(ext, first, coef, coef_plane, steps, planes, core, offset, count, base=None):
    _, rows, columns = ext.shape
    core_rows, core_columns = core

    def kernel(offset_ref, *refs):
        if base is None:
            u_ref, c_ref, o_ref = refs
        else:
            u_ref, c_ref, b_ref, o_ref = refs
        c = c_ref[0]
        face_x = c * pltpu.roll(c, rows - 1, 0)
        face_y = c * pltpu.roll(c, columns - 1, 1)

        def step(index, u):
            flux_x = face_x * (pltpu.roll(u, rows - 1, 0) - u)
            change_x = flux_x - pltpu.roll(flux_x, 1, 0)
            flux_y = face_y * (pltpu.roll(u, columns - 1, 1) - u)
            change_y = flux_y - pltpu.roll(flux_y, 1, 1)
            return u + change_x + change_y

        u = lax.fori_loop(0, steps, step, u_ref[0], unroll=True)
        kept = u[:core_rows, :core_columns]
        if base is None:
            o_ref[0] = kept
        else:
            o_ref[0] = b_ref[0] + kept

    def plane(p, offset_ref):
        return jnp.minimum(offset_ref[0] + p, planes - 1)

    in_specs = [
        pl.BlockSpec((1, rows, columns), lambda p, o: (p + first, 0, 0)),
        pl.BlockSpec((1, rows, columns), lambda p, o: (coef_plane(plane(p, o)), 0, 0)),
    ]
    operands = [ext, coef]
    if base is not None:
        in_specs.append(pl.BlockSpec((1, core_rows, core_columns), lambda p, o: (plane(p, o), 0, 0)))
        operands.append(base)
    grid_spec = pltpu.PrefetchScalarGridSpec(
        num_scalar_prefetch=1,
        grid=(count,),
        in_specs=in_specs,
        out_specs=pl.BlockSpec((1, core_rows, core_columns), lambda p, o: (p, 0, 0)),
    )
    return pl.pallas_call(
        kernel,
        grid_spec=grid_spec,
        out_shape=jax.ShapeDtypeStruct((count, core_rows, core_columns), jnp.float32),
    )(offset, *operands)


def exact_product(hot, values, contracting):
    high = values.astype(jnp.bfloat16)
    rest = values - high.astype(jnp.float32)
    middle = rest.astype(jnp.bfloat16)
    low = (rest - middle.astype(jnp.float32)).astype(jnp.bfloat16)
    width = values.shape[1]
    pieces = jnp.concatenate([high, middle, low], axis=1)
    numbers = (contracting, ((), ()))
    picked = lax.dot_general(hot, pieces, numbers, preferred_element_type=jnp.float32)
    return (picked[:, :width] + picked[:, width : 2 * width]) + picked[:, 2 * width :]


def gathered_shares(share, total):
    count = lax.axis_size("ma")
    here = lax.axis_index("ma").astype(jnp.int32)
    whole = jnp.zeros((count,) + share.shape, share.dtype)
    for steps in range(count):
        if steps == 0:
            piece = share
        else:
            piece = passed_along(share, "ma", steps)
        source = (here - steps) % count
        whole = lax.dynamic_update_index_in_dim(whole, piece, source, 0)
    head = whole[: count - 1].reshape(((count - 1) * share.shape[0],) + share.shape[1:])
    return jnp.concatenate([head, whole[count - 1, count * share.shape[0] - total :]], axis=0)


def summed_over_ma(value):
    count = lax.axis_size("ma")
    here = lax.axis_index("ma").astype(jnp.int32)
    whole = jnp.zeros((count,) + value.shape, value.dtype)
    for steps in range(count):
        piece = value if steps == 0 else passed_along(value, "ma", steps)
        whole = lax.dynamic_update_index_in_dim(whole, piece, (here - steps) % count, 0)
    total = whole[0]
    for index in range(1, count):
        total = total + whole[index]
    return total


def on_device(
    control, perturb, weights, kappa, wet_levels, obs_index, obs_count, innov, obs_weight
):
    planes, cells_x, cells_y = control.shape
    members = weights.shape[0]
    levels = (planes - 1) // 2
    core = (cells_x, cells_y)
    share = -(-planes // lax.axis_size("ma"))
    nominal_first = lax.axis_index("ma").astype(jnp.int32) * share
    first_plane = jnp.minimum(nominal_first, planes - share)
    offset = jnp.reshape(first_plane, (1,))
    no_offset = jnp.zeros((1,), jnp.int32)
    control_share = lax.dynamic_slice_in_dim(control, first_plane, share, 0)
    stack = jnp.concatenate(
        [control_share, weights, kappa, wet_levels.astype(jnp.float32)[None]], axis=0
    )
    ext = extended(stack, HALO)
    first_kappa = share + members
    kappa_ext = ext[first_kappa : first_kappa + 4]
    wet_ext = ext[first_kappa + 4]
    level_iota = lax.broadcasted_iota(jnp.int32, (levels, 1, 1), 0).astype(jnp.float32)
    wet_mask = (level_iota < wet_ext[None]).astype(jnp.float32)
    surface = wet_mask[0:1]
    coef = jnp.concatenate(
        [kappa_ext[0:1] * wet_mask, kappa_ext[1:2] * wet_mask, kappa_ext[2:3] * surface, kappa_ext[3:4] * surface],
        axis=0,
    )
    static_plane = lambda p: p
    local_plane = lambda p: planes
    member_scale = 1.0 / math.sqrt(members * lax.axis_size("ma"))
    static_share = diffuse_call(ext, 0, coef, static_plane, NSTEP, planes, core, offset, share)
    local = diffuse_call(ext, share, coef, local_plane, LSTEP, members, core, no_offset, members)
    partial_sum = member_scale * jnp.sum(perturb.astype(jnp.float32) * local[:, None], axis=0)
    cell_rows = planes * cells_x
    share_rows = share * cells_x
    row_of = obs_index // cells_y
    column_of = obs_index % cells_y
    row_hot = (row_of[:, None] == lax.broadcasted_iota(jnp.int32, (1, cell_rows), 1)).astype(jnp.bfloat16)
    column_hot = column_of[:, None] == lax.broadcasted_iota(jnp.int32, (1, cells_y), 1)
    plane_of = row_of // cells_x
    owned = (plane_of >= nominal_first) & (plane_of < nominal_first + share)
    share_row = jnp.where(owned, row_of - first_plane * cells_x, -1)
    share_hot = (share_row[:, None] == lax.broadcasted_iota(jnp.int32, (1, share_rows), 1)).astype(jnp.bfloat16)
    static_picked = exact_product(share_hot, static_share.reshape(share_rows, cells_y), ((1,), (0,)))
    partial_picked = exact_product(row_hot, partial_sum.reshape(cell_rows, cells_y), ((1,), (0,)))
    static_seen = jnp.sum(jnp.where(column_hot, static_picked, 0.0), axis=1)
    partial_seen = jnp.sum(jnp.where(column_hot, partial_picked, 0.0), axis=1)
    observed = summed_over_ma(static_seen + partial_seen)
    live_obs = lax.broadcasted_iota(jnp.int32, obs_index.shape, 0) < obs_count[0]
    misfit = obs_weight * (observed - innov)
    resid = jnp.where(live_obs, misfit, jnp.zeros_like(misfit))
    placed_resid = jnp.where(column_hot, resid[:, None], 0.0)
    adjoint = exact_product(row_hot, placed_resid, ((0,), (0,)))
    adjoint = adjoint.reshape(planes, cells_x, cells_y)
    project = member_scale * jnp.sum(perturb.astype(jnp.float32) * adjoint[None], axis=1)
    adjoint_share = lax.dynamic_slice_in_dim(adjoint, first_plane, share, 0)
    ext2 = extended(jnp.concatenate([adjoint_share, project], axis=0), HALO)
    grad_share = diffuse_call(ext2, 0, coef, static_plane, NSTEP, planes, core, offset, share, base=control)
    grad_control = gathered_shares(grad_share, planes)
    grad_weights = diffuse_call(ext2, share, coef, local_plane, LSTEP, members, core, no_offset, members, base=weights)
    return (grad_control, grad_weights)


def solution(mesh):
    placed = (
        P(None, "gx", "gy"),
        P("ma", None, "gx", "gy"),
        P("ma", "gx", "gy"),
        P(None, "gx", "gy"),
        P("gx", "gy"),
        P(("gx", "gy")),
        P(("gx", "gy")),
        P(("gx", "gy")),
        P(("gx", "gy")),
    )
    return jax.shard_map(
        on_device,
        mesh=mesh,
        in_specs=placed,
        out_specs=(P(None, "gx", "gy"), P("ma", "gx", "gy")),
        check_vma=False,
    )
```
